256 devices in a mesh: expert: 8 (over y, core), dp: 16 (over x, z_lo), tensor: 2 (over z_hi).
Axes of the slice: x: 4, y: 4, z: 8 (z_hi: 2, z_lo: 4; z = z_hi * 4 + z_lo), core: 2. Of those that a mesh axis runs over, the one named last changes fastest.
Arguments:
- tokens: bfloat16 [16384, 4096], P(('expert', 'dp'), 'tensor'), may hold values from -6 to 6
- grad_out: bfloat16 [16384, 4096], P(('expert', 'dp'), 'tensor'), may hold values from -6 to 6
- token_ids: int32 [16384], P(('expert', 'dp')), may hold values from 0 to 65535, as said below
- hash_table: int32 [65536], replicated, may hold values from 0 to 7, as said below
- gate_weight: bfloat16 [8, 4096, 768], P('expert', None, 'tensor'), may hold values from -0.09375 to 0.09375
- up_weight: bfloat16 [8, 4096, 768], P('expert', None, 'tensor'), may hold values from -0.09375 to 0.09375
- down_weight: bfloat16 [8, 4096, 768], P('expert', None, 'tensor'), may hold values from -0.21875 to 0.21875
Outputs:
- input_grad: bfloat16 [16384, 4096], P(('expert', 'dp'), 'tensor')
- gate_grad: float32 [8, 4096, 768], P('expert', 'dp', 'tensor')
- up_grad: float32 [8, 4096, 768], P('expert', 'dp', 'tensor')
- down_grad: float32 [8, 4096, 768], P('expert', 'dp', 'tensor')
The draws below stay inside these ranges and needn't reach their ends.
Inputs may be any that keep to these rules, and one draw needn't show every extreme that they name: `token_ids`: among the 128 tokens of one device (an aligned block of rows), at most 32 hash to any one expert. `hash_table`: each expert is the value of 8192 entries.
All inputs are finite; a program needn't handle non-finite values.
Results may differ from the reference program's by a relative error of at most 0.0059.
Values may be sent and summed in bfloat16 or wider, within the bound.
A program may use at most 128 MiB of HBM per device.

```python
import jax
import jax.numpy as jnp
from jax import lax

D = 4096
FF = 768
VOCAB = 65536
TOK_DEV = 128
EXPERTS = 8
GROUPS = 16
HIDDEN_BLOCKS = 2
CAP = 32
TOKENS = 16384
N_EXPERT = 8
N_DP = 16


def vocab_order(key):
    return jax.random.permutation(jax.random.fold_in(key, 101), VOCAB).astype(jnp.int32)


def draw_hash_table(key, part):
    return (vocab_order(key) % EXPERTS).astype(jnp.int32)


def draw_token_ids(key, part):
    order = vocab_order(key)
    inverse = jnp.zeros((VOCAB,), jnp.int32).at[order].set(jnp.arange(VOCAB, dtype=jnp.int32))
    blocks = TOKENS // TOK_DEV
    hot_group = jax.random.randint(jax.random.fold_in(key, 102), (GROUPS,), 0, EXPERTS).astype(jnp.int32)
    hot_block = hot_group[jnp.arange(blocks, dtype=jnp.int32) % GROUPS]
    position = jnp.arange(TOK_DEV, dtype=jnp.int32)
    others = (hot_block[:, None] + 1 + (position[None, :] - CAP) % (EXPERTS - 1)) % EXPERTS
    chosen = jnp.where(position[None, :] < CAP, hot_block[:, None], others)
    scores = jax.random.randint(jax.random.fold_in(key, 103), (blocks, TOK_DEV), 0, 1 << 20).astype(jnp.int32) * TOK_DEV + position[None, :]
    shuffle = jnp.argsort(scores, axis=1, stable=True)
    chosen = jnp.take_along_axis(chosen, shuffle, axis=1)
    column = jax.random.randint(jax.random.fold_in(key, 104), (blocks, TOK_DEV), 0, VOCAB // EXPERTS).astype(jnp.int32)
    return inverse[chosen + EXPERTS * column].reshape(TOKENS).astype(jnp.int32)


def shard_levels(key, dims, pieces, least, top_value):
    def one(axis_at, shards_of):
        draws = jax.random.uniform(jax.random.fold_in(jax.random.fold_in(key, 6), axis_at), (shards_of,), jnp.float32, least / len(pieces), top_value / len(pieces))
        return jnp.repeat(jnp.exp(draws), dims[axis_at] // shards_of).reshape((-1,) + (1,) * (len(dims) - axis_at - 1))

    gain = one(*pieces[0])
    for cut in pieces[1:]:
        gain = gain * one(*cut)
    return gain


def bell_draw(stream_key, extent, scale, bound, cuts=(), kind=jnp.bfloat16):
    factor_of = shard_levels(stream_key, extent, cuts, -0.22, 0.18) if cuts else 1.0
    result = jax.random.normal(stream_key, extent, jnp.float32) * scale * factor_of
    return jnp.minimum(jnp.maximum(result, -bound), bound).astype(kind)


def setup_inputs(seed: int = 0) -> dict:
    key_list = jax.random.split(jax.random.key(seed), 8)
    return {
        "tokens": bell_draw(key_list[0], (TOKENS, D), 1.0, 6.0, ((0, 128), (1, 2))),
        "grad_out": bell_draw(key_list[1], (TOKENS, D), 1.0, 6.0, ((0, 128), (1, 2))),
        "token_ids": draw_token_ids(jax.random.fold_in(key_list[7], 71), 0),
        "hash_table": draw_hash_table(jax.random.fold_in(key_list[7], 71), 0),
        "gate_weight": bell_draw(key_list[4], (EXPERTS, D, FF), D ** -0.5, 0.09375, ((0, 8), (2, 2))),
        "up_weight": bell_draw(key_list[5], (EXPERTS, D, FF), D ** -0.5, 0.09375, ((0, 8), (2, 2))),
        "down_weight": bell_draw(key_list[6], (EXPERTS, D, FF), FF ** -0.5, 0.21875, ((0, 8), (2, 2))),
    }


def reference(tokens, grad_out, token_ids, hash_table, gate_weight, up_weight, down_weight):
    route_of = jnp.take(hash_table, token_ids).astype(jnp.int32)
    total_rows = tokens.shape[0]
    most_rows = N_EXPERT * N_DP * CAP
    padded_tokens = jnp.concatenate([tokens, jnp.zeros((1, D), tokens.dtype)], 0)
    padded_grads = jnp.concatenate([grad_out, jnp.zeros((1, D), grad_out.dtype)], 0)
    block_width = FF // HIDDEN_BLOCKS
    mean_scale = 1.0 / TOK_DEV
    contract = (((0,), (0,)), ((), ()))

    def one_expert(expert_index):
        picks = jnp.nonzero(route_of == expert_index, size=most_rows, fill_value=total_rows)[0].astype(jnp.int32)
        rows_in = padded_tokens[picks]
        grads_in = padded_grads[picks]
        gate_matrix = gate_weight[expert_index]
        up_matrix = up_weight[expert_index]
        down_matrix = down_weight[expert_index]
        gate_value = jnp.dot(rows_in, gate_matrix, preferred_element_type=jnp.float32)
        lifted = jnp.dot(rows_in, up_matrix, preferred_element_type=jnp.float32)
        sigmoid_gate = jax.nn.sigmoid(gate_value)
        hidden = (gate_value * sigmoid_gate * lifted).astype(jnp.bfloat16)
        hidden_grad = jnp.dot(grads_in, down_matrix, preferred_element_type=jnp.float32)
        gate_delta = (hidden_grad * lifted * sigmoid_gate * (1.0 + gate_value * (1.0 - sigmoid_gate))).astype(jnp.bfloat16)
        up_delta = (hidden_grad * gate_value * sigmoid_gate).astype(jnp.bfloat16)
        summed = jnp.zeros((most_rows, D), jnp.float32)
        for block in range(HIDDEN_BLOCKS):
            low = block * block_width
            high = low + block_width
            term = jnp.dot(gate_delta[:, low:high], gate_matrix[:, low:high].T, preferred_element_type=jnp.float32)
            term = term + jnp.dot(up_delta[:, low:high], up_matrix[:, low:high].T, preferred_element_type=jnp.float32)
            rounded = lax.optimization_barrier(term.astype(jnp.bfloat16))
            summed = summed + rounded.astype(jnp.float32)
        input_rows = summed.astype(jnp.bfloat16)
        gate_part = lax.dot_general(rows_in, gate_delta, contract, preferred_element_type=jnp.float32) * mean_scale
        up_part = lax.dot_general(rows_in, up_delta, contract, preferred_element_type=jnp.float32) * mean_scale
        down_part = lax.dot_general(grads_in, hidden, contract, preferred_element_type=jnp.float32) * mean_scale
        return picks, input_rows, gate_part, up_part, down_part

    picks, input_rows, gate_grad, up_grad, down_grad = lax.map(one_expert, jnp.arange(EXPERTS, dtype=jnp.int32))
    input_grad = jnp.zeros((total_rows + 1, D), jnp.bfloat16)
    input_grad = input_grad.at[picks.reshape(-1)].set(input_rows.reshape(-1, D))[:total_rows]
    return input_grad, gate_grad, up_grad, down_grad
```

```python
import jax
import jax.numpy as jnp
from jax import lax
from jax.experimental import pallas as pl
from jax.experimental.pallas import tpu as pltpu
from jax.sharding import Mesh
from jax.sharding import PartitionSpec as P

TOK_DEV = 128
CAP = 32
NE = 8
TILE = 512


Z = ("zl", "zh")
E = ("y", "core")


def z_shift(a, by):
    def at(z):
        return (z % 4) * 2 + z // 4

    return lax.ppermute(a, Z, [(at(z), at((z + by) % 8)) for z in range(8)])


def e_shift(a, dy, dc):
    pairs = [(y * 2 + c, ((y + dy) % 4) * 2 + (c ^ dc)) for y in range(4) for c in range(2)]
    return lax.ppermute(a, E, pairs)


def x_shift(a, by):
    return lax.ppermute(a, "x", [(x, (x + by) % 4) for x in range(4)])


def zl_shift(a, by):
    return lax.ppermute(a, "zl", [(z, (z + by) % 4) for z in range(4)])


def dispatch_kernel(off_ref, slot_ref, a_ref, b_ref, *outs):
    rows = a_ref.shape[0]
    half = a_ref.shape[1]
    slots = NE * CAP
    pick = (lax.broadcasted_iota(jnp.int32, (slots, rows), 0) == slot_ref[...]).astype(jnp.bfloat16)
    for ref, at in ((a_ref, off_ref[0]), (b_ref, off_ref[1])):
        for t in range(half // TILE):
            got = jnp.dot(
                pick, ref[:, t * TILE : (t + 1) * TILE], preferred_element_type=jnp.float32
            ).astype(jnp.bfloat16)
            where = pl.ds(pl.multiple_of(at + t * TILE, TILE), TILE)
            for k in range(NE):
                outs[k][:, where] = got[k * CAP : (k + 1) * CAP]


def dispatch(offs, slot, a, b):
    width = 2 * a.shape[1]
    vmem = pl.BlockSpec(memory_space=pltpu.VMEM)
    return pl.pallas_call(
        dispatch_kernel,
        out_shape=[jax.ShapeDtypeStruct((CAP, width), jnp.bfloat16)] * NE,
        in_specs=[pl.BlockSpec(memory_space=pltpu.SMEM), vmem, vmem, vmem],
        out_specs=[vmem] * NE,
        cost_estimate=pl.CostEstimate(
            flops=2 * 256 * 128 * 4096, bytes_accessed=3 << 20, transcendentals=0
        ),
        name="dispatch",
    )(offs, slot, a, b)


def combine_kernel(off_ref, slot_ref, *refs):
    blocks, (a_ref, b_ref) = refs[:NE], refs[NE:]
    rows, half = a_ref.shape
    slots = NE * CAP
    pick = (lax.broadcasted_iota(jnp.int32, (rows, slots), 1) == slot_ref[...]).astype(jnp.bfloat16)
    for ref, at in ((a_ref, off_ref[0]), (b_ref, off_ref[1])):
        for t in range(half // TILE):
            where = pl.ds(pl.multiple_of(at + t * TILE, TILE), TILE)
            both = jnp.concatenate([blocks[k][:, where] for k in range(NE)], axis=0)
            ref[:, t * TILE : (t + 1) * TILE] = jnp.dot(
                pick, both, preferred_element_type=jnp.float32
            ).astype(jnp.bfloat16)


def combine(offs, slot, blocks, rows):
    half = blocks[0].shape[1] // 2
    vmem = pl.BlockSpec(memory_space=pltpu.VMEM)
    return pl.pallas_call(
        combine_kernel,
        out_shape=[jax.ShapeDtypeStruct((rows, half), jnp.bfloat16)] * 2,
        in_specs=[pl.BlockSpec(memory_space=pltpu.SMEM), vmem] + [vmem] * NE,
        out_specs=[vmem] * 2,
        cost_estimate=pl.CostEstimate(
            flops=2 * 256 * 128 * 4096, bytes_accessed=3 << 20, transcendentals=0
        ),
        name="combine",
    )(offs, slot, *blocks)


SHIFTS = [(k // 2, k % 2) for k in range(NE)]
ORDER = (4, 5, 2, 3, 6, 7, 1)


def sent_out(blocks):
    got = [blocks[0]] + [None] * (NE - 1)
    for k in ORDER:
        got[k] = e_shift(blocks[k], *SHIFTS[k])
    return got


def sent_back(blocks):
    got = [blocks[0]] + [None] * (NE - 1)
    for k in ORDER:
        dy, dc = SHIFTS[k]
        got[k] = e_shift(blocks[k], -dy, dc)
    return got


def rows_at(a, index, size):
    return lax.dynamic_slice_in_dim(a, index * size, size, axis=0)


def summed(part, x, zl):
    size = part.shape[0] // 4
    half = size // 2
    mine, ahead, across, behind = (rows_at(part, (x + d) % 4, size) for d in range(4))
    up = x_shift(across[:half], 1)
    down = x_shift(across[half:], -1)
    f32 = jnp.float32
    ahead = jnp.concatenate(
        [(ahead[:half].astype(f32) + up.astype(f32)).astype(jnp.bfloat16), ahead[half:]], axis=0
    )
    behind = jnp.concatenate(
        [behind[:half], (behind[half:].astype(f32) + down.astype(f32)).astype(jnp.bfloat16)], axis=0
    )
    from_low = x_shift(ahead, 1)
    from_high = x_shift(behind, -1)
    total = mine.astype(f32) + from_low.astype(f32) + from_high.astype(f32)
    rounded = total.astype(jnp.bfloat16)
    piece = size // 4
    out = rows_at(total, zl, piece)
    for d in (2, 1, 3):
        out = out + zl_shift(rows_at(rounded, (zl + d) % 4, piece), d).astype(f32)
    return out * (1.0 / TOK_DEV)


def local(tokens, grad_out, token_ids, hash_table, gate_weight, up_weight, down_weight):
    rows = tokens.shape[0]
    half_width = tokens.shape[1]
    bf16, f32 = jnp.bfloat16, jnp.float32
    x = lax.axis_index("x")
    zl = lax.axis_index("zl")
    z = lax.axis_index("zh") * 4 + zl
    y = lax.axis_index("y")
    core = lax.axis_index("core")
    ids = z_shift(token_ids, 2)
    tok_a = z_shift(tokens, 2)
    tok_b = z_shift(tokens, -2)
    grad_a = z_shift(grad_out, 2)
    grad_b = z_shift(grad_out, -2)
    off_a = jnp.where(jnp.logical_and(z >= 2, z < 6), 0, half_width).astype(jnp.int32)
    offs = jnp.stack([off_a, half_width - off_a])
    route_of = jnp.take(hash_table, ids)
    block_of = ((route_of // 2 - y) % 4) * 2 + jnp.bitwise_xor(route_of % 2, core)
    marked = (block_of[:, None] == jnp.arange(NE, dtype=jnp.int32)[None, :]).astype(jnp.int32)
    before = jnp.cumsum(marked, axis=0) - marked
    slot_of = block_of * CAP + jnp.sum(before * marked, axis=1)
    slot_row = slot_of[None, :]
    slot_col = slot_of[:, None]

    whole_tokens = jnp.concatenate(sent_out(dispatch(offs, slot_row, tok_a, tok_b)), axis=0)
    whole_grads = jnp.concatenate(sent_out(dispatch(offs, slot_row, grad_a, grad_b)), axis=0)

    gate_matrix = gate_weight[0]
    up_matrix = up_weight[0]
    down_matrix = down_weight[0]
    gate_value = jnp.dot(whole_tokens, gate_matrix, preferred_element_type=f32)
    lifted = jnp.dot(whole_tokens, up_matrix, preferred_element_type=f32)
    sigmoid_gate = jax.nn.sigmoid(gate_value)
    hidden = (gate_value * sigmoid_gate * lifted).astype(bf16)
    hidden_grad = jnp.dot(whole_grads, down_matrix, preferred_element_type=f32)
    gate_delta = (
        hidden_grad * lifted * sigmoid_gate * (1.0 + gate_value * (1.0 - sigmoid_gate))
    ).astype(bf16)
    up_delta = (hidden_grad * gate_value * sigmoid_gate).astype(bf16)
    contract = (((0,), (0,)), ((), ()))

    def weight_part(left, right):
        return lax.dot_general(left, right, contract, preferred_element_type=f32).astype(bf16)

    down_grad = summed(weight_part(whole_grads, hidden), x, zl)
    gate_grad = summed(weight_part(whole_tokens, gate_delta), x, zl)
    up_grad = summed(weight_part(whole_tokens, up_delta), x, zl)

    by_columns = (((1,), (1,)), ((), ()))
    partial_value = lax.dot_general(
        gate_delta, gate_matrix, by_columns, preferred_element_type=f32
    ) + lax.dot_general(up_delta, up_matrix, by_columns, preferred_element_type=f32)
    outgoing = partial_value.astype(bf16)
    back = sent_back([outgoing[k * CAP : (k + 1) * CAP] for k in range(NE)])
    ret_a, ret_b = combine(offs, slot_col, back, rows)
    input_grad = (z_shift(ret_a, -2).astype(f32) + z_shift(ret_b, 2).astype(f32)).astype(bf16)
    return (input_grad, gate_grad[None], up_grad[None], down_grad[None])


def solution(mesh):
    finer = Mesh(
        mesh.devices.reshape(4, 2, 4, 4, 2),
        ("y", "core", "x", "zl", "zh"),
    )
    spread = P(("y", "core", "x", "zl"), "zh")
    weight = P(("y", "core"), None, "zh")
    grads = P(("y", "core"), ("x", "zl"), "zh")
    return jax.shard_map(
        local,
        mesh=finer,
        in_specs=(spread, spread, P(("y", "core", "x", "zl")), P(), weight, weight, weight),
        out_specs=(spread, grads, grads, grads),
        check_vma=False,
    )
```

```python
import jax
import jax.numpy as jnp
from jax import lax
from jax.experimental import pallas as pl
from jax.experimental.pallas import tpu as pltpu
from jax.sharding import Mesh
from jax.sharding import PartitionSpec as P

TOK_DEV = 128
CAP = 32
NE = 8
TILE = 512


Z = ("zl", "zh")
E = ("y", "core")
MESH = pl.DeviceIdType.MESH


def z_shift(a, by):
    def at(z):
        return (z % 4) * 2 + z // 4

    return lax.ppermute(a, Z, [(at(z), at((z + by) % 8)) for z in range(8)])


def e_shift(a, dy, dc):
    pairs = [(y * 2 + c, ((y + dy) % 4) * 2 + (c ^ dc)) for y in range(4) for c in range(2)]
    return lax.ppermute(a, E, pairs)


def x_shift(a, by):
    return lax.ppermute(a, "x", [(x, (x + by) % 4) for x in range(4)])


def zl_shift(a, by):
    return lax.ppermute(a, "zl", [(z, (z + by) % 4) for z in range(4)])


def z_peer(by):
    z = lax.rem(lax.axis_index("zh") * 4 + lax.axis_index("zl") + (8 + by), 8)
    return {"zl": lax.rem(z, 4), "zh": lax.div(z, 4)}


def e_peer(k):
    y = lax.rem(lax.axis_index("y") + k // 2, 4)
    core = lax.rem(lax.axis_index("core") + k % 2, 2)
    return {"y": y, "core": core}


def greet(peers):
    barrier = pltpu.get_barrier_semaphore()
    for peer in peers:
        pl.semaphore_signal(barrier, inc=1, device_id=peer, device_id_type=MESH)
    pl.semaphore_wait(barrier, len(peers))


def remote(src, dst, send_sem, recv_sem, peer):
    return pltpu.make_async_remote_copy(
        src_ref=src,
        dst_ref=dst,
        send_sem=send_sem,
        recv_sem=recv_sem,
        device_id=peer,
        device_id_type=MESH,
    )


def dispatch_kernel(
    slot_ref, tok_ref, grad_ref, slot_out, xt_ref, xg_ref,
    zbuf, stage, slot_send, slot_recv, z_send, z_recv, y_send, y_recv,
):
    rows, half = tok_ref.shape
    slots = xt_ref.shape[0]
    chunks = half // TILE
    z_peers = (z_peer(2), z_peer(-2))
    peers = [None] + [e_peer(k) for k in range(1, NE)]
    greet(list(z_peers) + peers[1:])
    ids = remote(slot_ref, slot_out, slot_send, slot_recv, z_peers[0])
    ids.start()
    source = lax.div(lax.rem(lax.axis_index("zh") * 4 + lax.axis_index("zl") + 6, 8), 4)
    offs = (source * half, (1 - source) * half)

    def over_z(which, c, side):
        src = (tok_ref, grad_ref)[which]
        return remote(
            src.at[:, pl.ds(pl.multiple_of(c * TILE, TILE), TILE)],
            zbuf.at[which, side, c],
            z_send.at[which, side, c],
            z_recv.at[which, side, c],
            z_peers[side],
        )

    for which in range(2):

        def launch(c, carry):
            for side in range(2):
                over_z(which, c, side).start()
            return carry

        lax.fori_loop(0, chunks, launch, 0)

    ids.wait()
    pick = (
        lax.broadcasted_iota(jnp.int32, (slots, rows), 0) == slot_out[0:1, :]
    ).astype(jnp.bfloat16)

    for which in range(2):
        out = (xt_ref, xg_ref)[which]

        def route(c, carry):
            for side in range(2):
                over_z(which, c, side).wait_recv()
                got = jnp.dot(
                    pick, zbuf[which, side, c], preferred_element_type=jnp.float32
                ).astype(jnp.bfloat16)
                where = pl.ds(pl.multiple_of(offs[side] + c * TILE, TILE), TILE)
                out[0:CAP, where] = got[:CAP]
                stage[which, side, c] = got[CAP:]
            for side in range(2):
                where = pl.ds(pl.multiple_of(offs[side] + c * TILE, TILE), TILE)
                for k in ORDER:
                    remote(
                        stage.at[which, side, c, pl.ds((k - 1) * CAP, CAP)],
                        out.at[pl.ds(k * CAP, CAP), where],
                        y_send.at[which, k],
                        y_recv.at[which, k],
                        peers[k],
                    ).start()
            return carry

        lax.fori_loop(0, chunks, route, 0)

    for which in range(2):
        out = (xt_ref, xg_ref)[which]
        for k in ORDER:
            block = out.at[pl.ds(k * CAP, CAP)]
            remote(block, block, y_send.at[which, k], y_recv.at[which, k], peers[k]).wait()

        def finish(c, carry):
            for side in range(2):
                over_z(which, c, side).wait_send()
            return carry

        lax.fori_loop(0, chunks, finish, 0)


def dispatch(slot, tokens, grads):
    rows, half = tokens.shape
    slots = NE * CAP
    chunks = half // TILE
    bf16 = jnp.bfloat16
    vmem = pl.BlockSpec(memory_space=pltpu.VMEM)
    dma = pltpu.SemaphoreType.DMA
    return pl.pallas_call(
        dispatch_kernel,
        out_shape=[
            jax.ShapeDtypeStruct(slot.shape, jnp.int32),
            jax.ShapeDtypeStruct((slots, 2 * half), bf16),
            jax.ShapeDtypeStruct((slots, 2 * half), bf16),
        ],
        in_specs=[vmem] * 3,
        out_specs=[vmem] * 3,
        scratch_shapes=[
            pltpu.VMEM((2, 2, chunks, rows, TILE), bf16),
            pltpu.VMEM((2, 2, chunks, slots - CAP, TILE), bf16),
            dma,
            dma,
            dma((2, 2, chunks)),
            dma((2, 2, chunks)),
            dma((2, NE)),
            dma((2, NE)),
        ],
        compiler_params=pltpu.CompilerParams(collective_id=0, has_side_effects=True),
        name="dispatch",
    )(slot, tokens, grads)


def combine_kernel(off_ref, slot_ref, *refs):
    blocks, (a_ref, b_ref) = refs[:NE], refs[NE:]
    rows, half = a_ref.shape
    slots = NE * CAP
    pick = (lax.broadcasted_iota(jnp.int32, (rows, slots), 1) == slot_ref[...]).astype(jnp.bfloat16)
    for ref, at in ((a_ref, off_ref[0]), (b_ref, off_ref[1])):
        for t in range(half // TILE):
            where = pl.ds(pl.multiple_of(at + t * TILE, TILE), TILE)
            both = jnp.concatenate([blocks[k][:, where] for k in range(NE)], axis=0)
            ref[:, t * TILE : (t + 1) * TILE] = jnp.dot(
                pick, both, preferred_element_type=jnp.float32
            ).astype(jnp.bfloat16)


def combine(offs, slot, blocks, rows):
    half = blocks[0].shape[1] // 2
    vmem = pl.BlockSpec(memory_space=pltpu.VMEM)
    return pl.pallas_call(
        combine_kernel,
        out_shape=[jax.ShapeDtypeStruct((rows, half), jnp.bfloat16)] * 2,
        in_specs=[pl.BlockSpec(memory_space=pltpu.SMEM), vmem] + [vmem] * NE,
        out_specs=[vmem] * 2,
        cost_estimate=pl.CostEstimate(
            flops=2 * 256 * 128 * 4096, bytes_accessed=3 << 20, transcendentals=0
        ),
        name="combine",
    )(offs, slot, *blocks)


SHIFTS = [(k // 2, k % 2) for k in range(NE)]
ORDER = (4, 5, 2, 3, 6, 7, 1)


def sent_back(blocks):
    got = [blocks[0]] + [None] * (NE - 1)
    for k in ORDER:
        dy, dc = SHIFTS[k]
        got[k] = e_shift(blocks[k], -dy, dc)
    return got


def rows_at(a, index, size):
    return lax.dynamic_slice_in_dim(a, index * size, size, axis=0)


def summed(part, x, zl):
    size = part.shape[0] // 4
    half = size // 2
    mine, ahead, across, behind = (rows_at(part, (x + d) % 4, size) for d in range(4))
    up = x_shift(across[:half], 1)
    down = x_shift(across[half:], -1)
    f32 = jnp.float32
    ahead = jnp.concatenate(
        [(ahead[:half].astype(f32) + up.astype(f32)).astype(jnp.bfloat16), ahead[half:]], axis=0
    )
    behind = jnp.concatenate(
        [behind[:half], (behind[half:].astype(f32) + down.astype(f32)).astype(jnp.bfloat16)], axis=0
    )
    from_low = x_shift(ahead, 1)
    from_high = x_shift(behind, -1)
    total = mine.astype(f32) + from_low.astype(f32) + from_high.astype(f32)
    rounded = total.astype(jnp.bfloat16)
    piece = size // 4
    out = rows_at(total, zl, piece)
    for d in (2, 1, 3):
        out = out + zl_shift(rows_at(rounded, (zl + d) % 4, piece), d).astype(f32)
    return out * (1.0 / TOK_DEV)


def local(tokens, grad_out, token_ids, hash_table, gate_weight, up_weight, down_weight):
    rows = tokens.shape[0]
    half_width = tokens.shape[1]
    bf16, f32 = jnp.bfloat16, jnp.float32
    x = lax.axis_index("x")
    zl = lax.axis_index("zl")
    z = lax.axis_index("zh") * 4 + zl
    y = lax.axis_index("y")
    core = lax.axis_index("core")
    off_a = jnp.where(jnp.logical_and(z >= 2, z < 6), 0, half_width).astype(jnp.int32)
    offs = jnp.stack([off_a, half_width - off_a])
    route_of = jnp.take(hash_table, token_ids)
    block_of = ((route_of // 2 - y) % 4) * 2 + jnp.bitwise_xor(route_of % 2, core)
    marked = (block_of[:, None] == jnp.arange(NE, dtype=jnp.int32)[None, :]).astype(jnp.int32)
    before = jnp.cumsum(marked, axis=0) - marked
    slot_of = block_of * CAP + jnp.sum(before * marked, axis=1)
    slot_rows = jnp.broadcast_to(slot_of[None, :], (8, rows))
    their_slot, whole_tokens, whole_grads = dispatch(slot_rows, tokens, grad_out)
    slot_col = their_slot[0][:, None]

    gate_matrix = gate_weight[0]
    up_matrix = up_weight[0]
    down_matrix = down_weight[0]
    gate_value = jnp.dot(whole_tokens, gate_matrix, preferred_element_type=f32)
    lifted = jnp.dot(whole_tokens, up_matrix, preferred_element_type=f32)
    sigmoid_gate = jax.nn.sigmoid(gate_value)
    hidden = (gate_value * sigmoid_gate * lifted).astype(bf16)
    hidden_grad = jnp.dot(whole_grads, down_matrix, preferred_element_type=f32)
    gate_delta = (
        hidden_grad * lifted * sigmoid_gate * (1.0 + gate_value * (1.0 - sigmoid_gate))
    ).astype(bf16)
    up_delta = (hidden_grad * gate_value * sigmoid_gate).astype(bf16)
    contract = (((0,), (0,)), ((), ()))

    def weight_part(left, right):
        return lax.dot_general(left, right, contract, preferred_element_type=f32).astype(bf16)

    down_grad = summed(weight_part(whole_grads, hidden), x, zl)
    gate_grad = summed(weight_part(whole_tokens, gate_delta), x, zl)
    up_grad = summed(weight_part(whole_tokens, up_delta), x, zl)

    by_columns = (((1,), (1,)), ((), ()))
    partial_value = lax.dot_general(
        gate_delta, gate_matrix, by_columns, preferred_element_type=f32
    ) + lax.dot_general(up_delta, up_matrix, by_columns, preferred_element_type=f32)
    outgoing = partial_value.astype(bf16)
    back = sent_back([outgoing[k * CAP : (k + 1) * CAP] for k in range(NE)])
    ret_a, ret_b = combine(offs, slot_col, back, rows)
    input_grad = (z_shift(ret_a, -2).astype(f32) + z_shift(ret_b, 2).astype(f32)).astype(bf16)
    return (input_grad, gate_grad[None], up_grad[None], down_grad[None])


def solution(mesh):
    finer = Mesh(
        mesh.devices.reshape(4, 2, 4, 4, 2),
        ("y", "core", "x", "zl", "zh"),
    )
    spread = P(("y", "core", "x", "zl"), "zh")
    weight = P(("y", "core"), None, "zh")
    grads = P(("y", "core"), ("x", "zl"), "zh")
    return jax.shard_map(
        local,
        mesh=finer,
        in_specs=(spread, spread, P(("y", "core", "x", "zl")), P(), weight, weight, weight),
        out_specs=(spread, grads, grads, grads),
        check_vma=False,
    )
```

```python
import jax
import jax.numpy as jnp
from jax import lax
from jax.experimental import pallas as pl
from jax.experimental.pallas import tpu as pltpu
from jax.sharding import Mesh
from jax.sharding import PartitionSpec as P

TOK_DEV = 128
CAP = 32
NE = 8
TILE = 128
AHEAD = 4

MESH = pl.DeviceIdType.MESH
ORDER = (4, 5, 2, 3, 6, 7, 1)


def z_peer(by):
    z = lax.rem(lax.axis_index("zh") * 4 + lax.axis_index("zl") + (8 + by), 8)
    return {"zl": lax.rem(z, 4), "zh": lax.div(z, 4)}


def e_peer(k):
    y = lax.rem(lax.axis_index("y") + k // 2, 4)
    core = lax.rem(lax.axis_index("core") + k % 2, 2)
    return {"y": y, "core": core}


def greet(peers):
    barrier = pltpu.get_barrier_semaphore()
    for peer in peers:
        pl.semaphore_signal(barrier, inc=1, device_id=peer, device_id_type=MESH)
    pl.semaphore_wait(barrier, len(peers))


def remote(src, dst, send_sem, recv_sem, peer):
    return pltpu.make_async_remote_copy(
        src_ref=src,
        dst_ref=dst,
        send_sem=send_sem,
        recv_sem=recv_sem,
        device_id=peer,
        device_id_type=MESH,
    )


def dispatch_kernel(
    slot_ref, tok_ref, grad_ref, slot_out, xt_ref, xg_ref,
    zbuf, stage, slot_send, slot_recv, z_send, z_recv, y_send, y_recv,
):
    rows, half = tok_ref.shape
    slots = xt_ref.shape[0]
    chunks = half // TILE
    z_peers = (z_peer(2), z_peer(-2))
    peers = [None] + [e_peer(k) for k in range(1, NE)]
    greet(list(z_peers) + peers[1:])
    ids = remote(slot_ref, slot_out, slot_send, slot_recv, z_peers[0])
    ids.start()
    source = lax.div(lax.rem(lax.axis_index("zh") * 4 + lax.axis_index("zl") + 6, 8), 4)
    offs = (source * half, (1 - source) * half)

    def over_z(which, c, side):
        src = (tok_ref, grad_ref)[which]
        return remote(
            src.at[:, pl.ds(pl.multiple_of(c * TILE, TILE), TILE)],
            zbuf.at[which, side, c],
            z_send.at[which, side, c],
            z_recv.at[which, side, c],
            z_peers[side],
        )

    for c in range(AHEAD):
        for side in range(2):
            over_z(0, c, side).start()

    ids.wait()
    pick = (
        lax.broadcasted_iota(jnp.int32, (slots, rows), 0) == slot_out[0:1, :]
    ).astype(jnp.bfloat16)

    def route(which, c, following):
        out = (xt_ref, xg_ref)[which]
        for side in range(2):
            over_z(which, c, side).wait()
            if following is not None:
                over_z(*following, side).start()
        for side in range(2):
            got = jnp.dot(
                pick, zbuf[which, side, c], preferred_element_type=jnp.float32
            ).astype(jnp.bfloat16)
            where = pl.ds(pl.multiple_of(offs[side] + c * TILE, TILE), TILE)
            out[0:CAP, where] = got[:CAP]
            stage[which, side, c] = got[CAP:]
        for side in range(2):
            where = pl.ds(pl.multiple_of(offs[side] + c * TILE, TILE), TILE)
            for k in ORDER:
                remote(
                    stage.at[which, side, c, pl.ds((k - 1) * CAP, CAP)],
                    out.at[pl.ds(k * CAP, CAP), where],
                    y_send.at[which, k],
                    y_recv.at[which, k],
                    peers[k],
                ).start()

    for which in range(2):

        def step(c, carry):
            route(which, c, (which, c + AHEAD))
            return carry

        lax.fori_loop(0, chunks - AHEAD, step, 0)
        for c in range(chunks - AHEAD, chunks):
            route(which, c, (1, c - chunks + AHEAD) if which == 0 else None)

    for which in range(2):
        out = (xt_ref, xg_ref)[which]
        for k in ORDER:
            block = out.at[pl.ds(k * CAP, CAP)]
            remote(block, block, y_send.at[which, k], y_recv.at[which, k], peers[k]).wait()


def dispatch(slot, tokens, grads):
    rows, half = tokens.shape
    slots = NE * CAP
    chunks = half // TILE
    bf16 = jnp.bfloat16
    vmem = pl.BlockSpec(memory_space=pltpu.VMEM)
    dma = pltpu.SemaphoreType.DMA
    return pl.pallas_call(
        dispatch_kernel,
        out_shape=[
            jax.ShapeDtypeStruct(slot.shape, jnp.int32),
            jax.ShapeDtypeStruct((slots, 2 * half), bf16),
            jax.ShapeDtypeStruct((slots, 2 * half), bf16),
        ],
        in_specs=[vmem] * 3,
        out_specs=[vmem] * 3,
        scratch_shapes=[
            pltpu.VMEM((2, 2, chunks, rows, TILE), bf16),
            pltpu.VMEM((2, 2, chunks, slots - CAP, TILE), bf16),
            dma,
            dma,
            dma((2, 2, chunks)),
            dma((2, 2, chunks)),
            dma((2, NE)),
            dma((2, NE)),
        ],
        compiler_params=pltpu.CompilerParams(collective_id=0, has_side_effects=True),
        name="dispatch",
    )(slot, tokens, grads)


def x_peer(by):
    return {"x": lax.rem(lax.axis_index("x") + (4 + by), 4)}


def zl_peer(by):
    return {"zl": lax.rem(lax.axis_index("zl") + by, 4)}


DEPTHS = (2, 1, 3, 0)
PARTS = 4


def return_kernel(
    slot_ref, part_0, part_1, part_2, outgoing,
    in_grad, sum_0, sum_1, sum_2,
    own, low, high, low_in, high_in, first_up, first_down, z_out, z_in, back, ret, ret_in,
    load, f_send, f_recv, s_send, s_recv, z_send, z_recv, own_sem, y_send, y_recv, r_send, r_recv,
):
    f32, bf16 = jnp.float32, jnp.bfloat16
    parts = (part_0, part_1, part_2)
    sums = (sum_0, sum_1, sum_2)
    size = own.shape[1]
    half = size // 2
    piece = size // 4
    rows, half_width = in_grad.shape
    width = 2 * half_width
    cols = width // PARTS
    x = lax.axis_index("x")
    zl = lax.axis_index("zl")
    z = lax.axis_index("zh") * 4 + zl
    x_up, x_down = x_peer(1), x_peer(-1)
    z_back = (z_peer(-2), z_peer(2))
    lines = [None] + [zl_peer(d) for d in range(1, 4)]
    homes = [None] + [e_peer(((4 - k // 2) % 4) * 2 + k % 2) for k in range(1, NE)]
    source = lax.div(lax.rem(z + 6, 8), 4)
    offs = (source * half_width, (1 - source) * half_width)
    greet([x_up, x_down] + list(z_back) + lines[1:] + homes[1:])

    def chunk_of(m, d, at=0, count=None):
        start = lax.rem(x + d, 4) * size + at
        return parts[m].at[pl.ds(pl.multiple_of(start, half), count or size)]

    def first(m, up):
        if up:
            return remote(
                chunk_of(m, 2, 0, half), first_up.at[m], f_send.at[m, 0], f_recv.at[m, 0], x_up
            )
        return remote(
            chunk_of(m, 2, half, half), first_down.at[m], f_send.at[m, 1], f_recv.at[m, 1], x_down
        )

    def piece_at(d):
        return pl.ds(pl.multiple_of(lax.rem(zl + d, 4) * piece, piece), piece)

    def second(m, d, up):
        if up:
            return remote(
                low.at[m, piece_at(d)], low_in.at[m, piece_at(d)],
                s_send.at[m, d, 0], s_recv.at[m, d, 0], x_up,
            )
        return remote(
            high.at[m, piece_at(d)], high_in.at[m, piece_at(d)],
            s_send.at[m, d, 1], s_recv.at[m, d, 1], x_down,
        )

    def along_z(m, d):
        return remote(
            z_out.at[m, d - 1], z_in.at[m, d - 1], z_send.at[m, d - 1], z_recv.at[m, d - 1], lines[d]
        )

    def loads(m):
        return (
            pltpu.make_async_copy(chunk_of(m, 0), own.at[m], load.at[m, 0]),
            pltpu.make_async_copy(chunk_of(m, 1), low.at[m], load.at[m, 1]),
            pltpu.make_async_copy(chunk_of(m, 3), high.at[m], load.at[m, 2]),
        )

    def columns(c):
        at = offs[c % 2] + (c // 2) * cols
        return pl.ds(pl.multiple_of(at, cols), cols)

    def over_y(k, c):
        block = pl.ds(k * CAP, CAP)
        return remote(
            outgoing.at[block, columns(c)], back.at[block, columns(c)],
            y_send.at[k, c], y_recv.at[k, c], homes[k],
        )

    def over_z(c):
        return remote(ret.at[c], ret_in.at[c], r_send.at[c], r_recv.at[c], z_back[c % 2])

    def keep():
        return pltpu.make_async_copy(outgoing.at[pl.ds(0, CAP)], back.at[pl.ds(0, CAP)], own_sem)

    for m in range(2):
        first(m, True).start()
        first(m, False).start()
    for c in range(PARTS):
        for k in ORDER:
            over_y(k, c).start()
    keep().start()
    for m in range(3):
        for copy in loads(m):
            copy.start()

    def send_second(m):
        for copy in loads(m):
            copy.wait()
        first(m, True).wait_recv()
        top, bottom = pl.ds(0, half), pl.ds(half, half)
        low[m, top] = (low[m, top].astype(f32) + first_up[m].astype(f32)).astype(bf16)
        first(m, False).wait_recv()
        high[m, bottom] = (high[m, bottom].astype(f32) + first_down[m].astype(f32)).astype(bf16)
        for d in DEPTHS:
            second(m, d, True).start()
            second(m, d, False).start()

    pick = (
        lax.broadcasted_iota(jnp.int32, (rows, NE * CAP), 1) == slot_ref[...]
    ).astype(bf16)

    def send_home(c):
        for k in ORDER:
            over_y(k, c).wait_recv()
        ret[c] = jnp.dot(pick, back[:, columns(c)], preferred_element_type=f32).astype(bf16)
        over_z(c).start()

    def total(m, d):
        second(m, d, True).wait_recv()
        second(m, d, False).wait_recv()
        at = piece_at(d)
        both = (
            own[m, at].astype(f32) + low_in[m, at].astype(f32) + high_in[m, at].astype(f32)
        )
        if d == 0:
            sums[m][...] = both
        else:
            z_out[m, d - 1] = both.astype(bf16)
            along_z(m, d).start()

    def finish(m):
        out = sums[m][...]
        for d in DEPTHS[:3]:
            along_z(m, d).wait_recv()
            out = out + z_in[m, d - 1].astype(f32)
        sums[m][...] = out * (1.0 / TOK_DEV)

    keep().wait()
    send_second(0)
    first(2, True).start()
    first(2, False).start()
    send_home(0)
    send_home(1)
    send_second(1)
    send_home(2)
    send_home(3)
    for d in DEPTHS:
        total(0, d)
    send_second(2)
    for d in DEPTHS:
        total(1, d)
    for c in range(0, PARTS, 2):
        over_z(c).wait_recv()
        over_z(c + 1).wait_recv()
        in_grad[:, c // 2 * cols : (c // 2 + 1) * cols] = (
            ret_in[c].astype(f32) + ret_in[c + 1].astype(f32)
        ).astype(bf16)
    finish(0)
    for d in DEPTHS:
        total(2, d)
    finish(1)
    finish(2)
    for m in range(3):
        first(m, True).wait_send()
        first(m, False).wait_send()
        for d in range(4):
            second(m, d, True).wait_send()
            second(m, d, False).wait_send()
        for d in range(1, 4):
            along_z(m, d).wait_send()
    for c in range(PARTS):
        over_z(c).wait_send()
        for k in ORDER:
            over_y(k, c).wait_send()


def returned(slot_col, parts, outgoing):
    rows = slot_col.shape[0]
    slots, width = outgoing.shape
    depth, ff = parts[0].shape
    size = depth // 4
    cols = width // PARTS
    bf16, f32 = jnp.bfloat16, jnp.float32
    vmem = pl.BlockSpec(memory_space=pltpu.VMEM)
    anywhere = pl.BlockSpec(memory_space=pl.ANY)
    dma = pltpu.SemaphoreType.DMA
    return pl.pallas_call(
        return_kernel,
        out_shape=[jax.ShapeDtypeStruct((rows, width // 2), bf16)]
        + [jax.ShapeDtypeStruct((size // 4, ff), f32)] * 3,
        in_specs=[vmem] + [anywhere] * 4,
        out_specs=[vmem] * 4,
        scratch_shapes=[pltpu.VMEM((3, size, ff), bf16)] * 5
        + [pltpu.VMEM((3, size // 2, ff), bf16)] * 2
        + [pltpu.VMEM((3, 3, size // 4, ff), bf16)] * 2
        + [pltpu.VMEM((slots, width), bf16)]
        + [pltpu.VMEM((PARTS, rows, cols), bf16)] * 2
        + [
            dma((3, 3)),
            dma((3, 2)),
            dma((3, 2)),
            dma((3, 4, 2)),
            dma((3, 4, 2)),
            dma((3, 3)),
            dma((3, 3)),
            dma,
            dma((NE, PARTS)),
            dma((NE, PARTS)),
            dma((PARTS,)),
            dma((PARTS,)),
        ],
        compiler_params=pltpu.CompilerParams(collective_id=1, has_side_effects=True),
        name="return",
    )(slot_col, *parts, outgoing)


def local(tokens, grad_out, token_ids, hash_table, gate_weight, up_weight, down_weight):
    rows = tokens.shape[0]
    bf16, f32 = jnp.bfloat16, jnp.float32
    y = lax.axis_index("y")
    core = lax.axis_index("core")
    route_of = jnp.take(hash_table, token_ids)
    block_of = ((route_of // 2 - y) % 4) * 2 + jnp.bitwise_xor(route_of % 2, core)
    marked = (block_of[:, None] == jnp.arange(NE, dtype=jnp.int32)[None, :]).astype(jnp.int32)
    before = jnp.cumsum(marked, axis=0) - marked
    slot_of = block_of * CAP + jnp.sum(before * marked, axis=1)
    slot_rows = jnp.broadcast_to(slot_of[None, :], (8, rows))
    their_slot, whole_tokens, whole_grads = dispatch(slot_rows, tokens, grad_out)
    slot_col = their_slot[0][:, None]

    gate_matrix = gate_weight[0]
    up_matrix = up_weight[0]
    down_matrix = down_weight[0]
    gate_value = jnp.dot(whole_tokens, gate_matrix, preferred_element_type=f32)
    lifted = jnp.dot(whole_tokens, up_matrix, preferred_element_type=f32)
    sigmoid_gate = jax.nn.sigmoid(gate_value)
    hidden = (gate_value * sigmoid_gate * lifted).astype(bf16)
    hidden_grad = jnp.dot(whole_grads, down_matrix, preferred_element_type=f32)
    gate_delta = (
        hidden_grad * lifted * sigmoid_gate * (1.0 + gate_value * (1.0 - sigmoid_gate))
    ).astype(bf16)
    up_delta = (hidden_grad * gate_value * sigmoid_gate).astype(bf16)
    contract = (((0,), (0,)), ((), ()))

    def weight_part(left, right):
        return lax.dot_general(left, right, contract, preferred_element_type=f32).astype(bf16)

    down_part = weight_part(whole_grads, hidden)
    gate_part = weight_part(whole_tokens, gate_delta)
    up_part = weight_part(whole_tokens, up_delta)

    by_columns = (((1,), (1,)), ((), ()))
    partial_value = lax.dot_general(
        gate_delta, gate_matrix, by_columns, preferred_element_type=f32
    ) + lax.dot_general(up_delta, up_matrix, by_columns, preferred_element_type=f32)
    input_grad, down_grad, gate_grad, up_grad = returned(
        slot_col, (down_part, gate_part, up_part), partial_value.astype(bf16)
    )
    return (input_grad, gate_grad[None], up_grad[None], down_grad[None])


def solution(mesh):
    finer = Mesh(
        mesh.devices.reshape(4, 2, 4, 4, 2),
        ("y", "core", "x", "zl", "zh"),
    )
    spread = P(("y", "core", "x", "zl"), "zh")
    weight = P(("y", "core"), None, "zh")
    grads = P(("y", "core"), ("x", "zl"), "zh")
    return jax.shard_map(
        local,
        mesh=finer,
        in_specs=(spread, spread, P(("y", "core", "x", "zl")), P(), weight, weight, weight),
        out_specs=(spread, grads, grads, grads),
        check_vma=False,
    )
```
